32 devices in a mesh: space: 8 (over z, y), chan: 4 (over x, core).
Axes of the slice: x: 2, y: 2, z: 4, core: 2. Of those that a mesh axis runs over, the one named last changes fastest.
Arguments:
- feature_map: bfloat16 [32, 224, 1280], P('space', None, 'chan'), may hold values from -6 to 6
- conv_kernel: bfloat16 [9, 32, 1280], P(None, None, 'chan'), may hold values from -0.375 to 0.375
- weight_in: bfloat16 [1280, 5120], P(None, 'chan'), may hold values from -0.15625 to 0.15625
- weight_out: bfloat16 [5120, 1280], P('chan'), may hold values from -0.078125 to 0.078125
- cotangent: bfloat16 [32, 224, 1280], P('space', None, 'chan'), may hold values from -6 to 6
Outputs:
- block_out: bfloat16 [32, 224, 1280], P('space', None, 'chan')
- grad_features: bfloat16 [32, 224, 1280], P('space', None, 'chan')
- grad_kernel: float32 [9, 32, 1280], P(None, None, 'chan')
- grad_weight_in: float32 [1280, 5120], P(None, 'chan')
- grad_weight_out: float32 [5120, 1280], P('chan')
The draws below stay inside these ranges and needn't reach their ends.
All inputs are finite; a program needn't handle non-finite values.
Results may differ from the reference program's by a relative error of at most 0.019.
Values may be sent and summed in bfloat16 or wider, within the bound.
No kernel may reach another device: no remote copies, remote signals or barrier semaphores. Data moves between devices by JAX's collectives and lax.ppermute only.
A program may use at most 192 MiB of HBM per device.

```python
import math
import jax
import jax.numpy as jnp
from jax import lax

C = 1280
FF = 5120
GROUPS = 40
WIDTH = 224
HEIGHT = 32
N_CHAN = 4


def levels(key, shape, cuts, low, largest):
    def one(axis_at, shards_of):
        heights = jax.random.uniform(jax.random.fold_in(jax.random.fold_in(key, 6), axis_at), (shards_of,), jnp.float32, low / len(cuts), largest / len(cuts))
        return jnp.repeat(jnp.exp(heights), shape[axis_at] // shards_of).reshape((-1,) + (1,) * (len(shape) - axis_at - 1))

    level = one(*cuts[0])
    for cut in cuts[1:]:
        level = level * one(*cut)
    return level


def noise(own_key, extent, width, most, cuts=(), kind=jnp.bfloat16):
    level = levels(own_key, extent, cuts, -0.22, 0.18) if cuts else 1.0
    entries = jax.random.normal(own_key, extent, jnp.float32) * width * level
    return jnp.minimum(jnp.maximum(entries, -most), most).astype(kind)


def setup_inputs(seed: int = 0) -> dict:
    keys = jax.random.split(jax.random.key(seed), 6)
    feature_map = noise(keys[0], (HEIGHT, WIDTH, C), 1.0, 6.0, ((0, 8), (2, 4)))
    conv_kernel = noise(keys[1], (9, C // GROUPS, C), (9 * (C // GROUPS)) ** -0.5, 0.375, ((2, 4),))
    weight_in = noise(keys[2], (C, FF), C ** -0.5, 0.15625, ((1, 4),))
    weight_out = noise(keys[3], (FF, C), FF ** -0.5, 0.078125, ((0, 4),))
    cotangent = noise(keys[4], (HEIGHT, WIDTH, C), 1.0, 6.0, ((0, 8), (2, 4)))
    return dict(feature_map=feature_map, conv_kernel=conv_kernel, weight_in=weight_in, weight_out=weight_out, cotangent=cotangent)


def pad_map(field):
    return jnp.pad(field, ((1, 1), (1, 1), (0, 0)))

def group_conv(padded, kernel, row_count, col_count):
    width_group = kernel.shape[1]
    channels = kernel.shape[2]
    group_count = channels // width_group
    summed = jnp.zeros((row_count, col_count, group_count, width_group), jnp.float32)
    for tap_index in range(9):
        shift_row, shift_col = (tap_index // 3, tap_index % 3)
        window = padded[shift_row:shift_row + row_count, shift_col:shift_col + col_count]
        window = window.reshape(row_count, col_count, group_count, width_group).astype(jnp.float32)
        taps = kernel[tap_index].reshape(width_group, group_count, width_group).astype(jnp.float32)
        summed = summed + jnp.einsum('hwgj,jgo->hwgo', window, taps)
    return summed.reshape(row_count, col_count, channels)

def group_conv_t(padded, kernel, row_count, col_count):
    width_group = kernel.shape[1]
    channels = kernel.shape[2]
    group_count = channels // width_group
    summed = jnp.zeros((row_count, col_count, group_count, width_group), jnp.float32)
    for tap_index in range(9):
        shift_row, shift_col = (2 - tap_index // 3, 2 - tap_index % 3)
        window = padded[shift_row:shift_row + row_count, shift_col:shift_col + col_count]
        window = window.reshape(row_count, col_count, group_count, width_group).astype(jnp.float32)
        taps = kernel[tap_index].reshape(width_group, group_count, width_group).astype(jnp.float32)
        summed = summed + jnp.einsum('hwgo,jgo->hwgj', window, taps)
    return summed.reshape(row_count, col_count, channels)

def kernel_grad(padded, upstream, width_group, row_count, col_count):
    channels = upstream.shape[2]
    group_count = channels // width_group
    grads = []
    upper = upstream.reshape(row_count, col_count, group_count, width_group).astype(jnp.float32)
    for tap_index in range(9):
        shift_row, shift_col = (tap_index // 3, tap_index % 3)
        window = padded[shift_row:shift_row + row_count, shift_col:shift_col + col_count]
        window = window.reshape(row_count, col_count, group_count, width_group).astype(jnp.float32)
        grads.append(jnp.einsum('hwgj,hwgo->jgo', window, upper).reshape(width_group, channels))
    return jnp.stack(grads, axis=0)

def gelu_slope(values):
    return 0.5 * (1.0 + lax.erf(values / math.sqrt(2.0))) + values * jnp.exp(-0.5 * values * values) / math.sqrt(2.0 * math.pi)

def rounded(values):
    return lax.optimization_barrier(values.astype(jnp.bfloat16)).astype(jnp.float32)

def reference(feature_map, conv_kernel, weight_in, weight_out, cotangent):
    row_count, col_count, channels = feature_map.shape
    width_group = conv_kernel.shape[1]
    pixels = row_count * col_count
    block_hidden = FF // N_CHAN
    grad_scale = 1.0 / math.sqrt(pixels)
    padded = pad_map(feature_map)
    mixed = (feature_map.astype(jnp.float32) + group_conv(padded, conv_kernel, row_count, col_count)).astype(jnp.bfloat16)
    mixed_rows = mixed.reshape(pixels, channels)
    pre = jnp.dot(mixed_rows, weight_in, preferred_element_type=jnp.float32)
    hidden = jax.nn.gelu(pre, approximate=False).astype(jnp.bfloat16)
    mlp = jnp.zeros((pixels, channels), jnp.float32)
    for panel in range(N_CHAN):
        lower = panel * block_hidden
        mlp = mlp + rounded(jnp.dot(hidden[:, lower:lower + block_hidden], weight_out[lower:lower + block_hidden], preferred_element_type=jnp.float32))
    block_out = (mixed_rows.astype(jnp.float32) + mlp).astype(jnp.bfloat16).reshape(row_count, col_count, channels)
    cot_rows = cotangent.reshape(pixels, channels)
    grad_weight_out = jnp.dot(hidden.T, cot_rows, preferred_element_type=jnp.float32) * grad_scale
    dhidden = jnp.dot(cot_rows, weight_out.T, preferred_element_type=jnp.float32)
    dpre = (dhidden * gelu_slope(pre)).astype(jnp.bfloat16)
    grad_weight_in = jnp.dot(mixed_rows.T, dpre, preferred_element_type=jnp.float32) * grad_scale
    dmix = cot_rows.astype(jnp.float32)
    for panel in range(N_CHAN):
        lower = panel * block_hidden
        dmix = dmix + rounded(jnp.dot(dpre[:, lower:lower + block_hidden], weight_in[:, lower:lower + block_hidden].T, preferred_element_type=jnp.float32))
    dmixed = dmix.astype(jnp.bfloat16).reshape(row_count, col_count, channels)
    grad_features = (dmixed.astype(jnp.float32) + group_conv_t(pad_map(dmixed), conv_kernel, row_count, col_count)).astype(jnp.bfloat16)
    grad_kernel = kernel_grad(padded, dmixed, width_group, row_count, col_count) * grad_scale
    return (block_out, grad_features, grad_kernel, grad_weight_in, grad_weight_out)
```

```python
import functools
import math

import jax
import jax.numpy as jnp
from jax import lax
from jax.experimental import pallas as pl
from jax.experimental.pallas import tpu as pltpu
from jax.sharding import PartitionSpec as P

F32 = jnp.float32
BF16 = jnp.bfloat16
LANES = 128
SMEM = pl.BlockSpec(memory_space=pltpu.SMEM)


def flip(axis, bit):
    return [(i, i ^ bit) for i in range(lax.axis_size(axis))]


def dot(a, b, dims):
    return lax.dot_general(a, b, ((dims[:1], dims[1:]), ((), ())), preferred_element_type=F32)


def tie(*values):
    return lax.optimization_barrier(values)


def cost(microseconds):
    return pl.CostEstimate(flops=int(microseconds * 6e8), transcendentals=0, bytes_accessed=int(microseconds * 2e6))


def fixed(shape):
    return pl.BlockSpec(shape, lambda *_: (0,) * len(shape), pipeline_mode=pl.Buffered(1))


def up_lanes(size):
    return -(-size // LANES) * LANES


def halo(cells):
    count = lax.axis_size("space")
    above = lax.ppermute(cells[-1:], "space", [(i, i + 1) for i in range(count - 1)])
    below = lax.ppermute(cells[:1], "space", [(i + 1, i) for i in range(count - 1)])
    return above, below


def tile_kernel(kernel):
    taps, width, channels = kernel.shape
    lanes = up_lanes(channels)
    kernel = jnp.pad(kernel, ((0, 0), (0, 0), (0, lanes - channels)))
    tiled = jnp.tile(kernel, (1, LANES // width, 1))
    rows = lax.broadcasted_iota(jnp.int32, (LANES, lanes), 0) // width
    cols = (lax.broadcasted_iota(jnp.int32, (LANES, lanes), 1) % LANES) // width
    return jnp.where(rows == cols, tiled, jnp.zeros_like(tiled))


def fill_shifts(refs, shifted, columns):
    lanes = shifted.shape[2]
    base = 0
    for ref in refs:
        rows, _, channels = ref.shape
        size = rows * columns
        cells = ref[...].reshape(size, channels).astype(F32)
        if lanes != channels:
            cells = jnp.concatenate([cells, jnp.zeros((size, lanes - channels), F32)], axis=1)
        column = lax.broadcasted_iota(jnp.int32, (size, 1), 0) % columns
        left = jnp.where(column == 0, 0.0, pltpu.roll(cells, 1, 0))
        right = jnp.where(column == columns - 1, 0.0, pltpu.roll(cells, size - 1, 0))
        shifted[0, base : base + size, :] = left.astype(BF16)
        shifted[1, base : base + size, :] = cells.astype(BF16)
        shifted[2, base : base + size, :] = right.astype(BF16)
        base += size


def tap_sum(shifted, weights, tile, base, size, columns, turned):
    lanes = slice(tile * LANES, (tile + 1) * LANES)
    total = jnp.zeros((size, LANES), F32)
    for a in range(3):
        start = base + (2 - a if turned else a) * columns
        cells = jnp.concatenate(
            [shifted[2 - b if turned else b, start : start + size, lanes] for b in range(3)], axis=1
        )
        block = jnp.concatenate([weights[3 * a + b, :, lanes] for b in range(3)], axis=1 if turned else 0)
        total = total + dot(cells, block, (1, 1 if turned else 0))
    return total


def conv_part_body(count, offset, low_pixel, *refs):
    sources, weights, out_t, shifted = refs[:count], refs[count], refs[count + 1], refs[count + 2]
    columns = sources[0].shape[1]
    channels, size = out_t.shape
    fill_shifts(sources, shifted, columns)
    for tile in range(shifted.shape[2] // LANES):
        low = tile * LANES
        high = min(low + LANES, channels)
        start = low_pixel + offset
        centre = shifted[1, start : start + size, low : low + LANES].astype(F32)
        mixed = centre + tap_sum(shifted, weights, tile, start - columns, size, columns, False)
        out_t[low:high, :] = mixed.T[: high - low, :].astype(BF16)


def conv_part(sources, weights, offset, low_pixel, size):
    rows = sum(source.shape[0] for source in sources)
    _, columns, channels = sources[0].shape
    return pl.pallas_call(
        functools.partial(conv_part_body, len(sources), offset, low_pixel),
        out_shape=jax.ShapeDtypeStruct((channels, size), BF16),
        grid=(1,),
        in_specs=[fixed(x.shape) for x in (*sources, weights)],
        out_specs=fixed((channels, size)),
        scratch_shapes=[pltpu.VMEM((3, rows * columns, weights.shape[2]), BF16)],
        name="conv_part",
        cost_estimate=cost(4),
    )(*sources, weights)


def turned_body(above, cells, below, weights, out, shifted):
    rows, columns, channels = cells.shape
    size = rows * columns
    fill_shifts((above, cells, below), shifted, columns)
    for tile in range(shifted.shape[2] // LANES):
        low = tile * LANES
        high = min(low + LANES, channels)
        centre = shifted[1, columns : columns + size, low : low + LANES].astype(F32)
        total = centre + tap_sum(shifted, weights, tile, 0, size, columns, True)
        out[:, :, low:high] = total.astype(BF16).reshape(rows, columns, LANES)[:, :, : high - low]


def turned_conv(above, cells, below, weights):
    rows, columns, channels = cells.shape
    return pl.pallas_call(
        turned_body,
        grid=(1,),
        out_shape=jax.ShapeDtypeStruct(cells.shape, BF16),
        in_specs=[fixed(x.shape) for x in (above, cells, below, weights)],
        out_specs=fixed(cells.shape),
        scratch_shapes=[pltpu.VMEM((3, (rows + 2) * columns, weights.shape[2]), BF16)],
        name="turned_conv",
        cost_estimate=cost(5),
    )(above, cells, below, weights)


def tap_grad_body(above, cells, below, upstream_t, out, shifted):
    rows, columns, channels = cells.shape
    size = rows * columns
    width = out.shape[1]
    fill_shifts((above, cells, below), shifted, columns)
    group = lax.broadcasted_iota(jnp.int32, (1, LANES), 1) // width
    for tile in range(shifted.shape[2] // LANES):
        low = tile * LANES
        high = min(low + LANES, channels)
        upper = upstream_t[low:high, :]
        if high - low < LANES:
            upper = jnp.concatenate([upper, jnp.zeros((LANES - high + low, size), BF16)], axis=0)
        for a in range(3):
            cells_a = jnp.concatenate(
                [shifted[b, a * columns : a * columns + size, low : low + LANES] for b in range(3)], axis=1
            )
            found = dot(cells_a, upper, (0, 1))
            for b in range(3):
                total = jnp.zeros((width, LANES), F32)
                for g in range(LANES // width):
                    part = found[b * LANES + g * width : b * LANES + (g + 1) * width, :]
                    total = jnp.where(group == g, part, total)
                out[3 * a + b, :, low:high] = total[:, : high - low].astype(BF16)


def tap_grads(above, cells, below, upstream_t, width):
    rows, columns, channels = cells.shape
    return pl.pallas_call(
        tap_grad_body,
        grid=(1,),
        out_shape=jax.ShapeDtypeStruct((9, width, channels), BF16),
        in_specs=[fixed(x.shape) for x in (above, cells, below, upstream_t)],
        out_specs=fixed((9, width, channels)),
        scratch_shapes=[pltpu.VMEM((3, (rows + 2) * columns, up_lanes(channels)), BF16)],
        name="tap_grads",
        cost_estimate=cost(4),
    )(above, cells, below, upstream_t)


def cot_body(count, me_ref, w_out, *refs):
    pieces, (dhidden, cot, cot_all) = refs[:count], refs[count:]
    size = pieces[0].shape[0]

    @pl.when(pl.program_id(0) == 0)
    def _():
        for k in range(count):
            start = pl.multiple_of((me_ref[0] ^ k) * size, 16)
            cot_all[pl.ds(start, size), :] = pieces[k][...]

    dhidden[...] = jnp.dot(w_out[...], cot_all[...], preferred_element_type=F32)
    cut = cot.shape[1]
    start = pl.multiple_of(pl.program_id(0) * cut, 16)
    cot[...] = cot_all[pl.ds(start, cut), :].T


def cot_layer(me, weight_out, pieces):
    units, channels = weight_out.shape
    pixels = pieces[0].shape[1]
    block = math.gcd(units, 256)
    return pl.pallas_call(
        functools.partial(cot_body, len(pieces)),
        grid=(units // block,),
        out_shape=[jax.ShapeDtypeStruct((units, pixels), F32), jax.ShapeDtypeStruct((pixels, channels), BF16)],
        scratch_shapes=[pltpu.VMEM((channels, pixels), BF16)],
        in_specs=[SMEM, pl.BlockSpec((block, channels), lambda i: (i, 0))] + [fixed(x.shape) for x in pieces],
        out_specs=[
            pl.BlockSpec((block, pixels), lambda i: (i, 0)),
            pl.BlockSpec((pixels, channels * block // units), lambda i: (0, i)),
        ],
        name="cot_layer",
        cost_estimate=cost(8),
    )(me.reshape(1), weight_out, *pieces)


def hidden_body(count, me_ref, w_in, dhidden, *refs):
    firsts, seconds = refs[:count], refs[count : 2 * count]
    hidden, dpre, dpre_t, mixed_all = refs[2 * count :]
    size, split = firsts[0].shape

    @pl.when(pl.program_id(0) == 0)
    def _():
        for k in range(count):
            start = pl.multiple_of((me_ref[0] ^ k) * size, 16)
            mixed_all[pl.ds(start, size), :split] = firsts[k][...]
            mixed_all[pl.ds(start, size), split:] = seconds[k][...]

    pre = dot(w_in[...], mixed_all[...], (0, 0))
    gate = 0.5 * (1.0 + lax.erf(pre * (1.0 / math.sqrt(2.0))))
    hidden[...] = (pre * gate).astype(BF16)
    slope = gate + pre * jnp.exp(-0.5 * pre * pre) * (1.0 / math.sqrt(2.0 * math.pi))
    found = (dhidden[...] * slope).astype(BF16)
    dpre_t[...] = found
    dpre[...] = found.T


def hidden_layer(me, weight_in, dhidden, firsts, seconds):
    channels, units = weight_in.shape
    pixels = dhidden.shape[1]
    block = math.gcd(units, 256)
    rows = pl.BlockSpec((block, pixels), lambda i: (i, 0))
    return pl.pallas_call(
        functools.partial(hidden_body, len(firsts)),
        grid=(units // block,),
        out_shape=[
            jax.ShapeDtypeStruct((units, pixels), BF16),
            jax.ShapeDtypeStruct((pixels, units), BF16),
            jax.ShapeDtypeStruct((units, pixels), BF16),
            jax.ShapeDtypeStruct((channels, pixels), BF16),
        ],
        in_specs=[SMEM, pl.BlockSpec((channels, block), lambda i: (0, i)), rows]
        + [fixed(x.shape) for x in (*firsts, *seconds)],
        out_specs=[
            rows,
            pl.BlockSpec((pixels, block), lambda i: (0, i)),
            rows,
            pl.BlockSpec((channels, pixels), lambda i: (0, 0)),
        ],
        name="hidden_layer",
        cost_estimate=cost(10),
    )(me.reshape(1), weight_in, dhidden, *firsts, *seconds)


def back_body(w_in, dpre, out):
    out[...] = jnp.dot(w_in[...], dpre[...], preferred_element_type=F32).astype(BF16)


def forth_body(w_out, hidden, out):
    out[...] = dot(w_out[...], hidden[...], (0, 0)).astype(BF16)


def project(kernel, weight, values, along):
    units, pixels = values.shape
    channels = weight.shape[1 - along]
    block = math.gcd(channels, 256)
    shape = (block, units) if along else (units, block)
    return pl.pallas_call(
        kernel,
        grid=(channels // block,),
        out_shape=jax.ShapeDtypeStruct((channels, pixels), BF16),
        in_specs=[pl.BlockSpec(shape, (lambda i: (i, 0)) if along else (lambda i: (0, i))), fixed(values.shape)],
        out_specs=pl.BlockSpec((block, pixels), lambda i: (i, 0)),
        name="project_" + kernel.__name__,
        cost_estimate=cost(7),
    )(weight, values)


def blocks_body(index, hidden, mixed, cot, dpre, out, inner):
    out[...] = dot(hidden[...], cot[...], (1, 0)).astype(BF16)
    inner[...] = dot(mixed[...], dpre[...], (1, 0)).astype(BF16)


def stacked_blocks_body(*refs):
    blocks_body(*refs[:-1], refs[-1].at[0], refs[-1].at[1])


def grad_blocks(indices, count, hidden, mixed, cot, dpre):
    (units, pixels), channels = hidden.shape, cot.shape[1]
    out_rows, in_rows = units // count, channels // count
    index = jnp.stack([i % count for i in indices])

    def pick(rows):
        return pl.BlockSpec((None, rows, pixels), lambda i, at: (at[i], 0, 0))

    same = units == channels and len(indices) > 1
    if same:
        shapes = jax.ShapeDtypeStruct((len(indices), 2, out_rows, channels), BF16)
        specs = pl.BlockSpec((None, 2, out_rows, channels), lambda i, at: (i, 0, 0, 0))
    else:
        shapes = [
            jax.ShapeDtypeStruct((len(indices), out_rows, channels), BF16),
            jax.ShapeDtypeStruct((len(indices), in_rows, units), BF16),
        ]
        specs = [
            pl.BlockSpec((None, out_rows, channels), lambda i, at: (i, 0, 0)),
            pl.BlockSpec((None, in_rows, units), lambda i, at: (i, 0, 0)),
        ]
    found = pl.pallas_call(
        stacked_blocks_body if same else blocks_body,
        out_shape=shapes,
        grid_spec=pltpu.PrefetchScalarGridSpec(
            num_scalar_prefetch=1,
            grid=(len(indices),),
            in_specs=[pick(out_rows), pick(in_rows), fixed(cot.shape), fixed(dpre.shape)],
            out_specs=specs,
        ),
        name="grad_blocks",
        cost_estimate=cost(6),
    )(index, hidden.reshape(count, out_rows, pixels), mixed.reshape(count, in_rows, pixels), cot, dpre)
    if same or len(indices) == 1:
        return found
    return jnp.stack([found[0], found[1].reshape(found[0].shape)], axis=1)


def place_body(scale, index, out, inner, *refs):
    refs[-2][...] = out[...].astype(F32) * scale
    refs[-1][...] = inner[...].astype(F32) * scale


def place(parts, index, scale, held, out_shape, in_shape):
    rows = out_shape[1]
    cuts = 5 if rows % 80 == 0 and out_shape == in_shape else 1

    def spot(shape):
        return pl.BlockSpec((None, shape[1] // cuts, shape[2]), lambda i, at: (at[0], i, 0))

    whole = pl.BlockSpec(memory_space=pl.ANY)
    return pl.pallas_call(
        functools.partial(place_body, scale),
        out_shape=[jax.ShapeDtypeStruct(out_shape, F32), jax.ShapeDtypeStruct(in_shape, F32)],
        grid_spec=pltpu.PrefetchScalarGridSpec(
            num_scalar_prefetch=1,
            grid=(cuts,),
            in_specs=[
                pl.BlockSpec((None, x.shape[1] // cuts, x.shape[2]), lambda i, at, k=k: (k, i, 0)) for x, k in parts
            ]
            + [whole] * len(held),
            out_specs=[spot(out_shape), spot(in_shape)],
        ),
        input_output_aliases={3: 0, 4: 1} if held else {},
        name="place",
        cost_estimate=cost(2),
    )(index.reshape(1), *[x for x, _ in parts], *held)


def gather_chan(piece):
    pieces = []
    for k in range(lax.axis_size("chan") // 2):
        got = lax.ppermute(piece, "chan", flip("chan", 2 * k)) if k else piece
        pieces += [got, lax.ppermute(got, "chan", flip("chan", 1))]
    return pieces


def scatter_core(partial):
    count = lax.axis_size("chan")
    core = lax.axis_index("chan") % 2
    blocks = partial.reshape(count // 2, 2, partial.shape[0] // count, partial.shape[1])
    send = lax.dynamic_index_in_dim(blocks, 1 - core, 1, keepdims=False)
    keep = lax.dynamic_index_in_dim(blocks, core, 1, keepdims=False)
    got = lax.ppermute(send, "chan", flip("chan", 1))
    return (keep.astype(F32) + got.astype(F32)).astype(BF16)


def scatter_chip(pair):
    half = lax.axis_index("chan") // 2
    total = lax.dynamic_index_in_dim(pair, half, 0, keepdims=False).astype(F32)
    for k in range(1, pair.shape[0]):
        block = lax.dynamic_index_in_dim(pair, half ^ k, 0, keepdims=False)
        total = total + lax.ppermute(block, "chan", flip("chan", 2 * k)).astype(F32)
    return total


def ring_order(count):
    return list(range(0, count, 2)) + list(range(count - 1, 0, -2))


def body(feature_map, conv_kernel, weight_in, weight_out, cotangent):
    row_count, col_count, panel = feature_map.shape
    channels, units = weight_in.shape
    width = conv_kernel.shape[1]
    pixels = row_count * col_count
    count = lax.axis_size("space")
    grad_scale = 1.0 / math.sqrt(row_count * count * col_count)
    me = lax.axis_index("chan")

    cot_t, edges = tie(cotangent.reshape(pixels, panel).T, feature_map)
    cots = gather_chan(cot_t)
    above, below = tie(*halo(edges))
    weights = tile_kernel(conv_kernel)
    split = up_lanes(pixels // 2)
    mixed_a = conv_part((above, feature_map), weights, col_count, 0, split)
    pieces_a = gather_chan(mixed_a)
    mixed_b = conv_part((feature_map, below), weights, 0, split, pixels - split)
    pieces_b = gather_chan(mixed_b)
    dhidden, cot_all = cot_layer(me, weight_out, cots)
    hidden, dpre, dpre_t, mixed_all = hidden_layer(me, weight_in, dhidden, pieces_a, pieces_b)

    order = ring_order(count)
    spots = [0] * count
    for spot, device in enumerate(order):
        spots[device] = spot
    at = jnp.array(spots, jnp.int32)[lax.axis_index("space")] + count
    onward = [(order[i], order[(i + 1) % count]) for i in range(count)]
    backward = [(b, a) for a, b in onward]
    half = count // 2

    def shift(ahead, behind):
        return lax.ppermute(ahead, "space", onward), lax.ppermute(behind, "space", backward)

    def blocks(*indices, dpre=dpre):
        return grad_blocks(indices, count, hidden, mixed_all, cot_all, dpre)

    def plus(*values):
        return sum(value.astype(F32) for value in values).astype(BF16)

    ahead, behind = [x[0] for x in blocks(at + half)]
    behind = behind.reshape(ahead.shape)
    for step in range(1, half + 1):
        ahead, behind, dpre, dpre_t = tie(ahead, behind, dpre, dpre_t)
        got_ahead, got_behind = shift(ahead, behind)
        left = half - step
        if left:
            own = blocks(at + left, at - left, dpre=dpre)
            got_ahead, got_behind, own = tie(got_ahead, got_behind, own)
        else:
            own = [x[0] for x in blocks(at, dpre=dpre)]
            got_ahead, got_behind, *own = tie(got_ahead, got_behind, *own)
            own = jnp.stack([own[0], own[1].reshape(own[0].shape)])
        if step == half - 1:
            back = project(back_body, weight_in, dpre_t, 1)
            back_chip = scatter_chip(scatter_core(back))
        if step == 1:
            ahead = jnp.stack([plus(own[0, 0], got_ahead), own[0, 1]])
            behind = jnp.stack([own[1, 0], plus(own[1, 1], got_behind)])
        elif left:
            ahead, behind = plus(own[0], got_ahead), plus(own[1], got_behind)
        else:
            final = plus(own, got_ahead, got_behind)

    out_shape = (count, units // count, channels)
    in_shape = (count, channels // count, units)

    def put(held, block, index):
        outer, inner = block[0][None], block[1].reshape((1,) + in_shape[1:])
        if not held:
            return tuple(place(((outer, 0), (inner, 0)), index % count, grad_scale, (), out_shape, in_shape))
        return tuple(
            lax.dynamic_update_slice_in_dim(whole, part.astype(F32) * grad_scale, index % count, 0)
            for whole, part in zip(held, (outer, inner))
        )

    ahead = behind = final
    held = ()
    for step in range(1, half + 1):
        ahead, behind, hidden = tie(ahead, behind, hidden)
        if step < half:
            got_ahead, got_behind = shift(ahead, behind)
        else:
            got_ahead, got_behind = shift(ahead[0], behind[1])
        if step == 1:
            held = put(held, final, at)
        else:
            held = put(put(held, ahead, at - step + 1), behind, at + step - 1)
        got_ahead, got_behind, *held = tie(got_ahead, got_behind, *held)
        ahead, behind = got_ahead, got_behind
        if step == 1:
            mlp_chip = scatter_chip(scatter_core(project(forth_body, weight_out, hidden, 0)))
            dmixed_t = (cot_t.astype(F32) + back_chip).astype(BF16)
            dmixed = dmixed_t.T.reshape(row_count, col_count, panel)
            over, under = halo(dmixed)
            taps = tap_grads(above, feature_map, below, dmixed_t, width)
            bit = 1
            while bit < count:
                taps = plus(taps, lax.ppermute(taps, "space", flip("space", bit)))
                bit *= 2
        if step == min(2, half):
            ahead, behind, dmixed, over, under = tie(ahead, behind, dmixed, over, under)
            grad_features = turned_conv(over, dmixed, under, weights)
        if step == min(3, half):
            ahead, behind, mlp_chip = tie(ahead, behind, mlp_chip)
            mixed_t = jnp.concatenate([mixed_a, mixed_b], axis=1)
            block_out = (mixed_t.astype(F32) + mlp_chip).astype(BF16).T.reshape(row_count, col_count, panel)
            grad_conv = taps.astype(F32) * grad_scale
    grad_out, grad_in = put(held, jnp.stack([ahead, behind]), at + half)

    return block_out, grad_features, grad_conv, grad_in.reshape(channels, units), grad_out.reshape(units, channels)


def solution(mesh):
    return jax.shard_map(
        body,
        mesh=mesh,
        in_specs=(
            P("space", None, "chan"),
            P(None, None, "chan"),
            P(None, "chan"),
            P("chan", None),
            P("space", None, "chan"),
        ),
        out_specs=(
            P("space", None, "chan"),
            P("space", None, "chan"),
            P(None, None, "chan"),
            P(None, "chan"),
            P("chan", None),
        ),
        check_vma=False,
    )
```
